512 devices in a mesh: section: 16 (over x, y_hi, core), ctx: 32 (over z, y_lo).
Axes of the slice: x: 4, y: 4 (y_hi: 2, y_lo: 2; y = y_hi * 2 + y_lo), z: 16, core: 2. Of those that a mesh axis runs over, the one named last changes fastest.
Arguments:
- queries: bfloat16 [16, 4096, 4096], P('section', 'ctx'), may hold values from -8 to 8
- keys: bfloat16 [16, 4096, 512], P('section', 'ctx'), may hold values from -8 to 8
- values: bfloat16 [16, 4096, 512], P('section', 'ctx'), may hold values from -6 to 6
- token_pos: int32 [4096], P('ctx'), may hold values from 0 to 4095, as said below
- segment: int32 [4096], replicated, may hold values from 0 to 7, never falling along the last dimension, each value on 1 to 1024 neighbouring positions
Outputs:
- handed: bfloat16 [16, 4096, 4096], P('section', 'ctx')
The draws below stay inside these ranges and needn't reach their ends.
Inputs may be any that keep to these rules, and one draw needn't show every extreme that they name: `token_pos`: a permutation of the 4096 positions; the 128 rows of one index of ctx are two runs of 64 consecutive positions, starting at b * 64 and at (63 - b) * 64, each b used by one index. `segment`: document numbers never fall along the positions; each document covers 1 to 1024 positions, one exactly that many.
All inputs are finite; a program needn't handle non-finite values.
Results may differ from the reference program's by a relative error of at most 0.0059.
Values may be sent and summed in bfloat16 or wider, within the bound.
A program may use at most 64 MiB of HBM per device.

```python
import math
import jax
import jax.numpy as jnp
import numpy as np
from jax import lax

HEAD_SIZE = 128
QUERY_HEADS = 32
KEY_VALUE_HEADS = 4
TOK_DEV = 128
DOCS = 8
SEQUENCE_TOKENS = 4096
MICRO_BATCHES = 16


def draw_keys(key, part):
    root_random_key = jax.random.fold_in(key, 13)
    random_draw_result = jnp.clip(jax.random.normal(root_random_key, (MICRO_BATCHES, SEQUENCE_TOKENS, KEY_VALUE_HEADS * HEAD_SIZE), jnp.float32), -6.0, 6.0)
    return random_draw_result.astype(jnp.bfloat16)


def draw_queries(key, part):
    root_random_key = jax.random.fold_in(key, 21)
    random_draw_result = jnp.clip(jax.random.normal(root_random_key, (MICRO_BATCHES, SEQUENCE_TOKENS, QUERY_HEADS * HEAD_SIZE), jnp.float32), -6.0, 6.0)
    return random_draw_result.astype(jnp.bfloat16)


def draw_token_pos(key, part):
    block_count = SEQUENCE_TOKENS // TOK_DEV
    rows_per_half = TOK_DEV // 2
    block_order = jax.random.permutation(key, block_count)
    offsets = jnp.arange(rows_per_half)
    early_run = block_order[:, None] * rows_per_half + offsets[None, :]
    late_run = (2 * block_count - 1 - block_order)[:, None] * rows_per_half + offsets[None, :]
    return jnp.concatenate([early_run, late_run], axis=1).reshape(SEQUENCE_TOKENS).astype(jnp.int32)


def block_levels(key, shape, pieces, least, top_value):
    level = 1.0
    for dim, shards_of in pieces:
        draws = jax.random.uniform(jax.random.fold_in(jax.random.fold_in(key, 6), dim), (shards_of,), jnp.float32, least / len(pieces), top_value / len(pieces))
        level = level * jnp.repeat(jnp.exp(draws), shape[dim] // shards_of).reshape((-1,) + (1,) * (len(shape) - 1 - dim))
    return level


def profile(count, total, limit, lean):
    loads = [(1 << 20) // math.isqrt(rank ** lean) + 1 for rank in range(2, count + 1)]
    surplus, counts = total - limit - (count - 1), [1] * (count - 1)
    while surplus > 0:
        free = [i for i in range(count - 1) if counts[i] < limit]
        whole, left = sum([loads[i] for i in free]), surplus
        for i in free:
            more = min(limit - counts[i], max(1, left * loads[i] // whole), surplus)
            counts[i] = counts[i] + more
            surplus = surplus - more
    return np.array([limit] + counts)


def uneven_parts(stream_key, number_of, total, most, skew):
    if number_of == 2:
        one = jax.random.randint(stream_key, (), max(1, total - most), min(most, total - 1) + 1)
        return jnp.stack([one, total - one])
    tallies = jnp.asarray(profile(number_of, total, most, skew), jnp.int32)
    couples = (number_of - 1) // 2
    donor, taker = tallies[1:1 + 2 * couples:2], tallies[2:2 + 2 * couples:2]
    room = jnp.minimum(donor - 1, most - taker)
    moved = jax.random.randint(jax.random.fold_in(stream_key, 1), (couples,), 0, 1 << 20) % (room + 1)
    tallies = tallies.at[1:1 + 2 * couples:2].set(donor - moved).at[2:2 + 2 * couples:2].set(taker + moved)
    return tallies[jax.random.permutation(jax.random.fold_in(stream_key, 2), number_of)]


def scatter_about(own_key, dims, scale, limit, split=(), held_as=jnp.bfloat16):
    factor_of = block_levels(own_key, dims, split, -0.22, 0.18) if split else 1.0
    values = jax.random.normal(own_key, dims, jnp.float32) * scale * factor_of
    return jnp.minimum(jnp.maximum(values, -limit), limit).astype(held_as)


def setup_inputs(seed: int = 0) -> dict:
    splits = jax.random.split(jax.random.key(seed), 6)
    return {
        "queries": draw_queries(jax.random.fold_in(splits[5], 71), 0),
        "keys": draw_keys(jax.random.fold_in(splits[5], 71), 0),
        "values": scatter_about(splits[2], (MICRO_BATCHES, SEQUENCE_TOKENS, KEY_VALUE_HEADS * HEAD_SIZE), 1.0, 6.0, ((0, 16), (1, 32))),
        "token_pos": draw_token_pos(jax.random.fold_in(splits[5], 71), 0),
        "segment": jnp.searchsorted(jnp.cumsum(uneven_parts(splits[4], DOCS, SEQUENCE_TOKENS, SEQUENCE_TOKENS // 4, 2)), jnp.arange(SEQUENCE_TOKENS), side="right").astype(jnp.int32),
    }


def reference(queries, keys, values, token_pos, segment):
    inv_scale = 1.0 / math.sqrt(HEAD_SIZE)
    query_group_count = QUERY_HEADS // KEY_VALUE_HEADS
    doc_ids = jnp.take(segment, token_pos)
    allowed = (token_pos[None, :] <= token_pos[:, None]) & (doc_ids[None, :] == doc_ids[:, None])

    def one_head(operands):
        head_query, head_key, head_value = operands
        scores = jnp.dot(head_query.astype(jnp.float32), head_key.astype(jnp.float32).T, precision=lax.Precision.HIGHEST) * inv_scale
        scores = jnp.where(allowed, scores, jnp.float32(-1e+30))
        row_max = lax.optimization_barrier(jnp.max(scores, axis=1, keepdims=True))
        probabilities = jnp.where(allowed, jnp.exp(scores - row_max), jnp.float32(0.0))
        row_total = lax.optimization_barrier(jnp.sum(probabilities, axis=1, keepdims=True))
        weights = lax.optimization_barrier(probabilities.astype(jnp.bfloat16))
        summed = jnp.dot(weights.astype(jnp.float32), head_value.astype(jnp.float32), precision=lax.Precision.HIGHEST)
        return summed / row_total

    def one_section(operands):
        section_query, keys_of_section, values_of_section = operands
        head_queries = section_query.reshape(SEQUENCE_TOKENS, QUERY_HEADS, HEAD_SIZE).transpose(1, 0, 2)
        per_head_keys = jnp.repeat(keys_of_section.reshape(SEQUENCE_TOKENS, KEY_VALUE_HEADS, HEAD_SIZE).transpose(1, 0, 2), query_group_count, axis=0)
        per_head_values = jnp.repeat(values_of_section.reshape(SEQUENCE_TOKENS, KEY_VALUE_HEADS, HEAD_SIZE).transpose(1, 0, 2), query_group_count, axis=0)
        section_out = lax.map(one_head, (head_queries, per_head_keys, per_head_values))
        return section_out.transpose(1, 0, 2).reshape(SEQUENCE_TOKENS, QUERY_HEADS * HEAD_SIZE).astype(jnp.bfloat16)
    attended = lax.map(one_section, (queries, keys, values))
    return jnp.roll(attended, 1, axis=0)
```

```python
import functools
import math

import jax
import jax.numpy as jnp
from jax import lax
from jax.experimental import pallas as pl
from jax.experimental.pallas import tpu as pltpu
from jax.sharding import PartitionSpec as P

HEAD_SIZE = 128
QUERY_HEADS = 32
KEY_VALUE_HEADS = 4
DOCS = 8
GROUP = QUERY_HEADS // KEY_VALUE_HEADS
STAGES = KEY_VALUE_HEADS // 2
ROWS = 128
WIDE = GROUP * HEAD_SIZE
NEG = -1e30
MESH = pl.DeviceIdType.MESH


def kernel(
    sections,
    ring,
    q_hbm,
    k_hbm,
    v_hbm,
    pos_ref,
    seg_ref,
    out_hbm,
    kv,
    qbuf,
    obuf,
    posbuf,
    qrow,
    bias,
    vt,
    acc,
    top,
    total,
    loc_sem,
    par_send,
    par_recv,
    ring_send,
    ring_recv,
    pos_send,
    pos_recv,
    out_send,
    out_recv,
):
    groups = ring
    last = groups - 1
    sec = lax.axis_index("section")
    ctx = lax.axis_index("ctx")
    half = lax.rem(ctx, 2)
    mate = ctx + 1 - 2 * half
    right = lax.rem(ctx + 2, 2 * ring)
    left = lax.rem(ctx + 2 * ring - 2, 2 * ring)
    onward = lax.rem(sec + 1, sections)
    behind = lax.rem(sec + sections - 1, sections)
    toward = ((sec, right), (sec, left))

    def head_cols(which_half, stage):
        return pl.ds(pl.multiple_of((STAGES * which_half + stage) * HEAD_SIZE, HEAD_SIZE), HEAD_SIZE)

    def wide_cols(which_half, stage):
        return pl.ds(pl.multiple_of((STAGES * which_half + stage) * WIDE, WIDE), WIDE)

    local = []
    for stage in range(STAGES):
        local.append(
            (
                pltpu.make_async_copy(
                    k_hbm.at[0, :, head_cols(half, stage)], kv.at[stage, 0, 0, 0], loc_sem.at[stage, 0]
                ),
                pltpu.make_async_copy(
                    v_hbm.at[0, :, head_cols(half, stage)], kv.at[stage, 0, 1, 0], loc_sem.at[stage, 1]
                ),
                pltpu.make_async_copy(
                    q_hbm.at[0, :, wide_cols(half, stage)],
                    qbuf.at[stage, pl.ds(0, ROWS), :],
                    loc_sem.at[stage, 2],
                ),
            )
        )
    for copies in local:
        for copy in copies:
            copy.start()
    posbuf[0] = pos_ref[...].astype(jnp.float32)

    def swap(stage):
        return (
            pltpu.make_async_remote_copy(
                k_hbm.at[0, :, head_cols(1 - half, stage)],
                kv.at[stage, 0, 0, 1],
                par_send.at[stage, 0],
                par_recv.at[stage, 0],
                device_id=(sec, mate),
                device_id_type=MESH,
            ),
            pltpu.make_async_remote_copy(
                v_hbm.at[0, :, head_cols(1 - half, stage)],
                kv.at[stage, 0, 1, 1],
                par_send.at[stage, 1],
                par_recv.at[stage, 1],
                device_id=(sec, mate),
                device_id_type=MESH,
            ),
            pltpu.make_async_remote_copy(
                q_hbm.at[0, :, wide_cols(1 - half, stage)],
                qbuf.at[stage, pl.ds(ROWS, ROWS), :],
                par_send.at[stage, 2],
                par_recv.at[stage, 2],
                device_id=(sec, mate),
                device_id_type=MESH,
            ),
        )

    def ring_copy(stage, from_group, from_side, group, way):
        return pltpu.make_async_remote_copy(
            kv.at[stage, from_group, :, from_side],
            kv.at[stage, group, :, way],
            ring_send.at[stage, group, way],
            ring_recv.at[stage, group, way],
            device_id=toward[way],
            device_id_type=MESH,
        )

    def pos_copy(from_slot, group, way, device):
        slot = 2 * group + way
        return pltpu.make_async_remote_copy(
            posbuf.at[from_slot],
            posbuf.at[slot],
            pos_send.at[slot],
            pos_recv.at[slot],
            device_id=device,
            device_id_type=MESH,
        )

    mate_pos = pos_copy(0, 0, 1, (sec, mate))

    barrier = pltpu.get_barrier_semaphore()
    greeted = (
        (sec, mate),
        (sec, right),
        (sec, left),
        (onward, ctx),
        (onward, mate),
        (behind, ctx),
        (behind, mate),
    )
    for device in greeted:
        pl.semaphore_signal(barrier, inc=1, device_id=device, device_id_type=MESH)
    pl.semaphore_wait(barrier, len(greeted))

    swap_a = swap(0)
    swap_a[0].start()
    swap_a[1].start()
    mate_pos.start()

    def launch(stage, side):
        for way in range(2):
            ring_copy(stage, 0, side, 1 + side, way).start()
            if stage == 0:
                pos_copy(side, 1 + side, way, toward[way]).start()

    def arrive(stage, group, way):
        ring_copy(stage, 0, 0, group, way).wait_recv()
        if stage == 0:
            pos_copy(0, group, way, toward[way]).wait_recv()

    def pass_on(stage, group, into, way):
        ring_copy(stage, group, way, into, way).start()
        if stage == 0:
            pos_copy(2 * group + way, into, way, toward[way]).start()

    def take(stage, group):
        arrive(stage, group, 0)
        if isinstance(group, int):
            if group <= last - 2:
                pass_on(stage, group, group + 2, 0)
        else:
            pass_on(stage, group, group + 2, 0)
        arrive(stage, group, 1)
        if isinstance(group, int):
            if group <= last - 3:
                pass_on(stage, group, group + 2, 1)
            elif group == last - 1:
                pass_on(stage, group, last, 1)
        else:
            pass_on(stage, group, group + 2, 1)

    local[0][0].wait()
    local[0][1].wait()
    launch(0, 0)
    swap_a[2].start()
    swap_a[0].wait_recv()
    swap_a[1].wait_recv()
    mate_pos.wait_recv()
    launch(0, 1)

    place = jnp.concatenate([posbuf[0], posbuf[1]], axis=1)
    first = jnp.zeros_like(place)
    for doc in range(1, DOCS):
        count = jnp.sum((seg_ref[...] < doc).astype(jnp.float32), axis=0, keepdims=True)
        begin = jnp.sum(count, axis=1, keepdims=True)
        first = jnp.maximum(first, jnp.where(begin <= place, begin, 0.0))
    qrow[0] = place
    qrow[1] = first

    scale = math.log2(math.e) / math.sqrt(HEAD_SIZE)

    def attend(stage, group, finish=False):
        for way in range(2):
            spot = jnp.transpose(jnp.broadcast_to(posbuf[2 * group + way], (ROWS, ROWS)))
            for side in range(2):
                lanes = slice(side * ROWS, (side + 1) * ROWS)
                allowed = (spot <= qrow[0, :, lanes]) & (spot >= qrow[1, :, lanes])
                bias[way * ROWS : (way + 1) * ROWS, lanes] = jnp.where(allowed, 0.0, NEG)
            vt[:, way * ROWS : (way + 1) * ROWS] = jnp.transpose(kv[stage, group, 1, way])
        key_rows = kv[stage, group, 0].reshape(2 * ROWS, HEAD_SIZE)
        for head in range(GROUP):
            cols = slice(head * HEAD_SIZE, (head + 1) * HEAD_SIZE)
            scores = lax.dot_general(
                key_rows,
                qbuf[stage, :, cols],
                (((1,), (1,)), ((), ())),
                preferred_element_type=jnp.float32,
            )
            scores = scores * scale + bias[...]
            old = top[head]
            new = jnp.maximum(old, jnp.max(scores, axis=0, keepdims=True))
            probabilities = jnp.exp2(scores - new)
            factor = jnp.exp2(old - new)
            row_total = total[head] * factor + jnp.sum(probabilities, axis=0, keepdims=True)
            weighted = acc[head] * factor + jnp.dot(
                vt[...], probabilities.astype(jnp.bfloat16), preferred_element_type=jnp.float32
            )
            if finish:
                result = jnp.transpose(weighted * (1.0 / row_total))
                obuf[stage, :, cols] = result.astype(jnp.bfloat16)
                for side in range(2):
                    hand(stage, head, side).start()
            else:
                top[head] = new
                total[head] = row_total
                acc[head] = weighted

    def hand(stage, head, side):
        spot = pl.multiple_of(((STAGES * half + stage) * GROUP + head) * HEAD_SIZE, HEAD_SIZE)
        return pltpu.make_async_remote_copy(
            obuf.at[stage, pl.ds(side * ROWS, ROWS), pl.ds(head * HEAD_SIZE, HEAD_SIZE)],
            out_hbm.at[0, :, pl.ds(spot, HEAD_SIZE)],
            out_send.at[stage, head, side],
            out_recv.at[stage, head, side],
            device_id=(onward, ctx if side == 0 else mate),
            device_id_type=MESH,
        )

    def start_stage():
        top[...] = jnp.full_like(top, NEG)
        total[...] = jnp.zeros_like(total)
        acc[...] = jnp.zeros_like(acc)

    swap_b = swap(1)

    start_stage()
    idle = min(5, last - 3)
    pairs = max(0, min(last - 3, 2 * idle + 1) - idle)

    def passing(group, carry):
        take(0, group)
        return carry

    lax.fori_loop(1, idle + 1, passing, 0)
    for copy in swap_b:
        copy.start()
    local[0][2].wait()
    swap_a[2].wait_recv()

    def catching_up(group, carry):
        take(0, group)

        def one(index, carry):
            attend(0, 2 * (group - idle - 1) + index)
            return carry

        return lax.fori_loop(0, 2, one, carry)

    lax.fori_loop(idle + 1, idle + pairs + 1, catching_up, 0)
    done = 2 * pairs
    local[1][0].wait()
    local[1][1].wait()

    def working(stage):
        def step(group, carry):
            attend(stage, group)
            return carry

        return step

    for group in range(idle + pairs + 1, last + 1):
        take(0, group)
        if group == last - 2:
            launch(1, 0)
        if group == last - 1:
            swap_b[0].wait_recv()
            swap_b[1].wait_recv()
            launch(1, 1)
        until = min(group + 1, last)
        lax.fori_loop(done, until, working(0), 0)
        done = until
    attend(0, last, finish=True)

    start_stage()
    local[1][2].wait()
    swap_b[2].wait_recv()

    def both(group, carry):
        attend(1, group)
        take(1, group + 1)
        return carry

    lax.fori_loop(0, last - 3, both, 0)
    for group in range(last - 3, last):
        lax.fori_loop(group, group + 1, working(1), 0)
        take(1, group + 1)
    attend(1, last, finish=True)

    for copy in swap_a + swap_b + (mate_pos,):
        copy.wait_send()

    def sent(group, carry):
        for way in range(2):
            for stage in range(STAGES):
                ring_copy(stage, 0, 0, group, way).wait_send()
            pos_copy(0, group, way, toward[way]).wait_send()
        return carry

    lax.fori_loop(1, groups, sent, 0)

    for stage in range(STAGES):
        for head in range(GROUP):
            for side in range(2):
                copy = hand(stage, head, side)
                copy.wait_send()
                copy.wait_recv()


def per_device(sections, ring, queries, keys, values, token_pos, segment):
    anywhere = pl.BlockSpec(memory_space=pl.ANY)
    inside = pl.BlockSpec(memory_space=pltpu.VMEM)
    dma = pltpu.SemaphoreType.DMA
    pairs = ROWS * 2 * ring * ROWS * 2 * QUERY_HEADS // 2
    return pl.pallas_call(
        functools.partial(kernel, sections, ring),
        out_shape=jax.ShapeDtypeStruct(queries.shape, jnp.bfloat16),
        in_specs=[anywhere, anywhere, anywhere, inside, inside],
        out_specs=anywhere,
        scratch_shapes=[
            pltpu.VMEM((STAGES, ring, 2, 2, ROWS, HEAD_SIZE), jnp.bfloat16),
            pltpu.VMEM((STAGES, 2 * ROWS, WIDE), jnp.bfloat16),
            pltpu.VMEM((STAGES, 2 * ROWS, WIDE), jnp.bfloat16),
            pltpu.VMEM((2 * ring, 1, ROWS), jnp.float32),
            pltpu.VMEM((2, 1, 2 * ROWS), jnp.float32),
            pltpu.VMEM((2 * ROWS, 2 * ROWS), jnp.float32),
            pltpu.VMEM((HEAD_SIZE, 2 * ROWS), jnp.bfloat16),
            pltpu.VMEM((GROUP, HEAD_SIZE, 2 * ROWS), jnp.float32),
            pltpu.VMEM((GROUP, 1, 2 * ROWS), jnp.float32),
            pltpu.VMEM((GROUP, 1, 2 * ROWS), jnp.float32),
            dma((STAGES, 3)),
            dma((STAGES, 3)),
            dma((STAGES, 3)),
            dma((STAGES, ring, 2)),
            dma((STAGES, ring, 2)),
            dma((2 * ring,)),
            dma((2 * ring,)),
            dma((STAGES, GROUP, 2)),
            dma((STAGES, GROUP, 2)),
        ],
        compiler_params=pltpu.CompilerParams(
            collective_id=0, has_side_effects=True, vmem_limit_bytes=48 * 1024 * 1024
        ),
        cost_estimate=pl.CostEstimate(
            flops=4 * HEAD_SIZE * pairs, bytes_accessed=4 * 1024 * 1024, transcendentals=pairs
        ),
    )(queries, keys, values, token_pos.reshape(1, ROWS), segment.reshape(-1, 128))


def solution(mesh):
    return jax.shard_map(
        functools.partial(per_device, mesh.shape["section"], mesh.shape["ctx"] // 2),
        mesh=mesh,
        in_specs=(
            P("section", "ctx", None),
            P("section", "ctx", None),
            P("section", "ctx", None),
            P("ctx"),
            P(),
        ),
        out_specs=P("section", "ctx", None),
        check_vma=False,
    )
```

```python
import functools
import math

import jax
import jax.numpy as jnp
from jax import lax
from jax.experimental import pallas as pl
from jax.experimental.pallas import tpu as pltpu
from jax.sharding import PartitionSpec as P

HEAD_SIZE = 128
QUERY_HEADS = 32
KEY_VALUE_HEADS = 4
DOCS = 8
GROUP = QUERY_HEADS // KEY_VALUE_HEADS
STAGES = KEY_VALUE_HEADS // 2
ROWS = 128
WIDE = GROUP * HEAD_SIZE
NEG = -1e30
MESH = pl.DeviceIdType.MESH


def kernel(
    sections,
    ring,
    q_hbm,
    k_hbm,
    v_hbm,
    pos_hbm,
    seg_hbm,
    out_hbm,
    kv,
    qbuf,
    obuf,
    pos_ref,
    seg_ref,
    posbuf,
    qrow,
    bias,
    vt,
    acc,
    top,
    total,
    loc_sem,
    par_send,
    par_recv,
    ring_send,
    ring_recv,
    pos_send,
    pos_recv,
    out_send,
    out_recv,
):
    hops = ring // 2
    sec = lax.axis_index("section")
    ctx = lax.axis_index("ctx")
    half = lax.rem(ctx, 2)
    mate = ctx + 1 - 2 * half
    right = lax.rem(ctx + 2, 2 * ring)
    left = lax.rem(ctx + 2 * ring - 2, 2 * ring)
    onward = lax.rem(sec + 1, sections)
    behind = lax.rem(sec + sections - 1, sections)
    toward = ((sec, right), (sec, left))

    def head_cols(which_half, stage):
        return pl.ds(pl.multiple_of((STAGES * which_half + stage) * HEAD_SIZE, HEAD_SIZE), HEAD_SIZE)

    def wide_cols(which_half, stage):
        return pl.ds(pl.multiple_of((STAGES * which_half + stage) * WIDE, WIDE), WIDE)

    local = []
    for stage in range(STAGES):
        local.append(
            (
                pltpu.make_async_copy(
                    k_hbm.at[0, :, head_cols(half, stage)], kv.at[stage, 0, 0, 0], loc_sem.at[stage, 0]
                ),
                pltpu.make_async_copy(
                    v_hbm.at[0, :, head_cols(half, stage)], kv.at[stage, 0, 1, 0], loc_sem.at[stage, 1]
                ),
                pltpu.make_async_copy(
                    q_hbm.at[0, :, wide_cols(half, stage)],
                    qbuf.at[stage, pl.ds(0, ROWS), :],
                    loc_sem.at[stage, 2],
                ),
            )
        )
    small = (
        pltpu.make_async_copy(pos_hbm, pos_ref, loc_sem.at[0, 3]),
        pltpu.make_async_copy(seg_hbm, seg_ref, loc_sem.at[1, 3]),
    )
    for copy in small + local[0] + local[1]:
        copy.start()
    small[0].wait()
    posbuf[0] = pos_ref[...].astype(jnp.float32)

    def swap(stage):
        return (
            pltpu.make_async_remote_copy(
                k_hbm.at[0, :, head_cols(1 - half, stage)],
                kv.at[stage, 0, 0, 3],
                par_send.at[stage, 0],
                par_recv.at[stage, 0],
                device_id=(sec, mate),
                device_id_type=MESH,
            ),
            pltpu.make_async_remote_copy(
                v_hbm.at[0, :, head_cols(1 - half, stage)],
                kv.at[stage, 0, 1, 3],
                par_send.at[stage, 1],
                par_recv.at[stage, 1],
                device_id=(sec, mate),
                device_id_type=MESH,
            ),
            pltpu.make_async_remote_copy(
                q_hbm.at[0, :, wide_cols(1 - half, stage)],
                qbuf.at[stage, pl.ds(ROWS, ROWS), :],
                par_send.at[stage, 2],
                par_recv.at[stage, 2],
                device_id=(sec, mate),
                device_id_type=MESH,
            ),
        )

    def ring_copy(stage, hop, from_piece, piece):
        return pltpu.make_async_remote_copy(
            kv.at[stage, hop, :, from_piece],
            kv.at[stage, hop + 1, :, piece],
            ring_send.at[stage, hop + 1, piece],
            ring_recv.at[stage, hop + 1, piece],
            device_id=toward[piece % 2],
            device_id_type=MESH,
        )

    def pos_copy(from_slot, slot, device):
        return pltpu.make_async_remote_copy(
            posbuf.at[from_slot],
            posbuf.at[slot],
            pos_send.at[slot],
            pos_recv.at[slot],
            device_id=device,
            device_id_type=MESH,
        )

    mate_pos = pos_copy(0, 3, (sec, mate))

    barrier = pltpu.get_barrier_semaphore()
    greeted = (
        (sec, mate),
        (sec, right),
        (sec, left),
        (onward, ctx),
        (onward, mate),
        (behind, ctx),
        (behind, mate),
    )
    for device in greeted:
        pl.semaphore_signal(barrier, inc=1, device_id=device, device_id_type=MESH)
    pl.semaphore_wait(barrier, len(greeted))

    swap_a = swap(0)
    swap_a[0].start()
    swap_a[1].start()
    mate_pos.start()

    def send(stage, hop, from_piece, piece):
        ring_copy(stage, hop, from_piece, piece).start()

        @pl.when(stage == 0)
        def _():
            pos_copy(4 * hop + from_piece, 4 * hop + 4 + piece, toward[piece % 2]).start()

    def launch(stage, side):
        for way in range(2):
            send(stage, 0, 3 * side, 2 * side + way)

    def take(stage, hop):
        for piece in range(4) if not (isinstance(hop, int) and hop == hops) else (0, 3):
            ring_copy(stage, hop - 1, 0, piece).wait_recv()

            @pl.when(stage == 0)
            def _():
                pos_copy(0, 4 * hop + piece, toward[piece % 2]).wait_recv()

            if isinstance(hop, int):
                if hop < hops - 1 or (hop == hops - 1 and piece in (0, 3)):
                    send(stage, hop, piece, piece)
            elif piece in (0, 3):
                send(stage, hop, piece, piece)
            else:

                @pl.when(hop < hops - 1)
                def _():
                    send(stage, hop, piece, piece)

    local[0][0].wait()
    local[0][1].wait()
    launch(0, 0)
    swap_a[2].start()
    swap_a[0].wait_recv()
    swap_a[1].wait_recv()
    mate_pos.wait_recv()
    launch(0, 1)

    small[1].wait()

    place = jnp.concatenate([posbuf[0], posbuf[3]], axis=1)
    first = jnp.zeros_like(place)
    for doc in range(1, DOCS):
        count = jnp.sum((seg_ref[...] < doc).astype(jnp.float32), axis=0, keepdims=True)
        begin = jnp.sum(count, axis=1, keepdims=True)
        first = jnp.maximum(first, jnp.where(begin <= place, begin, 0.0))
    qrow[0] = place
    qrow[1] = first

    scale = math.log2(math.e) / math.sqrt(HEAD_SIZE)

    def attend(stage, hop, pieces=(0, 1, 2, 3), finish=False):
        width = len(pieces) * ROWS

        @pl.when(stage == 0)
        def _():
            for at, piece in enumerate(pieces):
                spot = jnp.transpose(jnp.broadcast_to(posbuf[4 * hop + piece], (ROWS, ROWS)))
                for side in range(2):
                    lanes = slice(side * ROWS, (side + 1) * ROWS)
                    allowed = (spot <= qrow[0, :, lanes]) & (spot >= qrow[1, :, lanes])
                    bias[hop, at * ROWS : (at + 1) * ROWS, lanes] = jnp.where(allowed, 0.0, NEG)

        for at, piece in enumerate(pieces):
            vt[:, at * ROWS : (at + 1) * ROWS] = jnp.transpose(kv[stage, hop, 1, piece])
        key_rows = jnp.concatenate([kv[stage, hop, 0, piece] for piece in pieces], axis=0)

        def score(head):
            return lax.dot_general(
                key_rows,
                qbuf[stage, :, head * HEAD_SIZE : (head + 1) * HEAD_SIZE],
                (((1,), (1,)), ((), ())),
                preferred_element_type=jnp.float32,
            )

        def soften(head, scores):
            scores = scores * scale + bias[hop, :width]
            old = top[stage, head]
            new = jnp.maximum(old, jnp.max(scores, axis=0, keepdims=True))
            probabilities = jnp.exp2(scores - new)
            factor = jnp.exp2(old - new)
            total[stage, head] = total[stage, head] * factor + jnp.sum(
                probabilities, axis=0, keepdims=True
            )
            top[stage, head] = new
            return probabilities.astype(jnp.bfloat16), factor

        def weigh(head, probabilities, factor):
            weighted = acc[stage, head] * factor + jnp.dot(
                vt[:, :width], probabilities, preferred_element_type=jnp.float32
            )
            if finish:
                result = jnp.transpose(weighted * (1.0 / total[stage, head]))
                obuf[stage, :, head * HEAD_SIZE : (head + 1) * HEAD_SIZE] = result.astype(
                    jnp.bfloat16
                )
                for side in range(2):
                    hand(stage, head, side).start()
            else:
                acc[stage, head] = weighted

        scores, behind_by_one = score(0), None
        for head in range(GROUP):
            following = score(head + 1) if head + 1 < GROUP else None
            softened = soften(head, scores)
            if behind_by_one is not None:
                weigh(head - 1, *behind_by_one)
            scores, behind_by_one = following, softened
        weigh(GROUP - 1, *behind_by_one)

    def hand(stage, head, side):
        spot = pl.multiple_of(((STAGES * half + stage) * GROUP + head) * HEAD_SIZE, HEAD_SIZE)
        return pltpu.make_async_remote_copy(
            obuf.at[stage, pl.ds(side * ROWS, ROWS), pl.ds(head * HEAD_SIZE, HEAD_SIZE)],
            out_hbm.at[0, :, pl.ds(spot, HEAD_SIZE)],
            out_send.at[stage, head, side],
            out_recv.at[stage, head, side],
            device_id=(onward, ctx if side == 0 else mate),
            device_id_type=MESH,
        )

    swap_b = swap(1)
    ends = (0, 3)

    def first_hop_of_b():
        for copy in swap_b:
            copy.start()
        local[1][0].wait()
        local[1][1].wait()
        launch(1, 0)
        swap_b[0].wait_recv()
        swap_b[1].wait_recv()
        launch(1, 1)

    top[...] = jnp.full_like(top, NEG)
    total[...] = jnp.zeros_like(total)
    acc[...] = jnp.zeros_like(acc)
    take(0, 1)
    first_hop_of_b()
    if hops == 8:
        take(0, 2)
        take(1, 1)
        local[0][2].wait()
        swap_a[2].wait_recv()
        attend(0, 0, ends)

        def early(index, carry):
            attend(0, index)
            stage = lax.rem(index + 1, 2)
            take(stage, (index + 5) // 2 - stage)
            return carry

        lax.fori_loop(1, 5, early, 0)
        local[1][2].wait()
        swap_b[2].wait_recv()
        attend(1, 0, ends)

        def late(index, carry):
            turn, which = index // 3, lax.rem(index, 3)
            stage = lax.rem(which + 1, 2)
            attend(stage, stage * (2 * turn + 1 + which // 2) + (1 - stage) * (5 + turn))

            @pl.when(which < 2)
            def _():
                take(which, 5 + turn - which)

            return carry

        lax.fori_loop(0, 9, late, 0)
        take(0, 8)
        take(1, 7)
        attend(0, 8, ends, finish=True)
        attend(1, 7)
        take(1, 8)
        attend(1, 8, ends, finish=True)
    else:
        local[0][2].wait()
        swap_a[2].wait_recv()
        local[1][2].wait()
        swap_b[2].wait_recv()
        for stage in range(STAGES):
            attend(stage, 0, ends)
        take(1, 1)
        for hop in range(1, hops):
            for stage in range(STAGES):
                attend(stage, hop)
                take(stage, hop + 1)
        for stage in range(STAGES):
            attend(stage, hops, ends, finish=True)

    for copy in swap_a + swap_b + (mate_pos,):
        copy.wait_send()

    def sent(hop, pieces):
        for piece in pieces:
            for stage in range(STAGES):
                ring_copy(stage, hop - 1, 0, piece).wait_send()
            pos_copy(0, 4 * hop + piece, toward[piece % 2]).wait_send()

    def all_sent(hop, carry):
        sent(hop, range(4))
        return carry

    lax.fori_loop(1, hops, all_sent, 0)
    sent(hops, ends)

    for stage in range(STAGES):
        for head in range(GROUP):
            for side in range(2):
                copy = hand(stage, head, side)
                copy.wait_send()
                copy.wait_recv()


def per_device(sections, ring, queries, keys, values, token_pos, segment):
    anywhere = pl.BlockSpec(memory_space=pl.ANY)
    dma = pltpu.SemaphoreType.DMA
    hops = ring // 2
    pairs = ROWS * 2 * ring * ROWS * 2 * QUERY_HEADS // 2
    return pl.pallas_call(
        functools.partial(kernel, sections, ring),
        out_shape=jax.ShapeDtypeStruct(queries.shape, jnp.bfloat16),
        in_specs=[anywhere] * 5,
        out_specs=anywhere,
        scratch_shapes=[
            pltpu.VMEM((STAGES, hops + 1, 2, 4, ROWS, HEAD_SIZE), jnp.bfloat16),
            pltpu.VMEM((STAGES, 2 * ROWS, WIDE), jnp.bfloat16),
            pltpu.VMEM((STAGES, 2 * ROWS, WIDE), jnp.bfloat16),
            pltpu.VMEM((1, ROWS), jnp.int32),
            pltpu.VMEM((ring * ROWS * 2 // 128, 128), jnp.int32),
            pltpu.VMEM((4 * hops + 4, 1, ROWS), jnp.float32),
            pltpu.VMEM((2, 1, 2 * ROWS), jnp.float32),
            pltpu.VMEM((hops + 1, 4 * ROWS, 2 * ROWS), jnp.float32),
            pltpu.VMEM((HEAD_SIZE, 4 * ROWS), jnp.bfloat16),
            pltpu.VMEM((STAGES, GROUP, HEAD_SIZE, 2 * ROWS), jnp.float32),
            pltpu.VMEM((STAGES, GROUP, 1, 2 * ROWS), jnp.float32),
            pltpu.VMEM((STAGES, GROUP, 1, 2 * ROWS), jnp.float32),
            dma((STAGES, 4)),
            dma((STAGES, 3)),
            dma((STAGES, 3)),
            dma((STAGES, hops + 1, 4)),
            dma((STAGES, hops + 1, 4)),
            dma((4 * hops + 4,)),
            dma((4 * hops + 4,)),
            dma((STAGES, GROUP, 2)),
            dma((STAGES, GROUP, 2)),
        ],
        compiler_params=pltpu.CompilerParams(
            collective_id=0, has_side_effects=True, vmem_limit_bytes=60 * 1024 * 1024
        ),
        cost_estimate=pl.CostEstimate(
            flops=4 * HEAD_SIZE * pairs, bytes_accessed=4 * 1024 * 1024, transcendentals=pairs
        ),
    )(queries, keys, values, token_pos.reshape(1, ROWS), segment.reshape(-1, 128))


def solution(mesh):
    return jax.shard_map(
        functools.partial(per_device, mesh.shape["section"], mesh.shape["ctx"] // 2),
        mesh=mesh,
        in_specs=(
            P("section", "ctx", None),
            P("section", "ctx", None),
            P("section", "ctx", None),
            P("ctx"),
            P(),
        ),
        out_specs=P("section", "ctx", None),
        check_vma=False,
    )
```

```python
import functools
import math

import jax
import jax.numpy as jnp
from jax import lax
from jax.experimental import pallas as pl
from jax.experimental.pallas import tpu as pltpu
from jax.sharding import PartitionSpec as P

HEAD_SIZE = 128
QUERY_HEADS = 32
KEY_VALUE_HEADS = 4
DOCS = 8
GROUP = QUERY_HEADS // KEY_VALUE_HEADS
STAGES = KEY_VALUE_HEADS // 2
ROWS = 128
WIDE = GROUP * HEAD_SIZE
NEG = -1e30
MESH = pl.DeviceIdType.MESH


def kernel(
    sections,
    ring,
    q_hbm,
    k_hbm,
    v_hbm,
    pos_hbm,
    seg_hbm,
    out_hbm,
    kv,
    qbuf,
    obuf,
    pos_ref,
    seg_ref,
    posbuf,
    qrow,
    bias,
    vt,
    acc,
    top,
    total,
    loc_sem,
    par_send,
    par_recv,
    ring_send,
    ring_recv,
    pos_send,
    pos_recv,
    out_send,
    out_recv,
):
    hops = ring // 2
    sec = lax.axis_index("section")
    ctx = lax.axis_index("ctx")
    half = lax.rem(ctx, 2)
    mate = ctx + 1 - 2 * half
    right = lax.rem(ctx + 2, 2 * ring)
    left = lax.rem(ctx + 2 * ring - 2, 2 * ring)
    onward = lax.rem(sec + 1, sections)
    behind = lax.rem(sec + sections - 1, sections)
    toward = ((sec, right), (sec, left))

    def head_cols(which_half, stage):
        return pl.ds(pl.multiple_of((STAGES * which_half + stage) * HEAD_SIZE, HEAD_SIZE), HEAD_SIZE)

    def wide_cols(which_half, stage):
        return pl.ds(pl.multiple_of((STAGES * which_half + stage) * WIDE, WIDE), WIDE)

    local = []
    for stage in range(STAGES):
        local.append(
            (
                pltpu.make_async_copy(
                    k_hbm.at[0, :, head_cols(half, stage)], kv.at[stage, 0, 0, 0], loc_sem.at[stage, 0]
                ),
                pltpu.make_async_copy(
                    v_hbm.at[0, :, head_cols(half, stage)], kv.at[stage, 0, 1, 0], loc_sem.at[stage, 1]
                ),
                pltpu.make_async_copy(
                    q_hbm.at[0, :, wide_cols(half, stage)],
                    qbuf.at[stage, pl.ds(0, ROWS), :],
                    loc_sem.at[stage, 2],
                ),
            )
        )
    small = (
        pltpu.make_async_copy(pos_hbm, pos_ref, loc_sem.at[0, 3]),
        pltpu.make_async_copy(seg_hbm, seg_ref, loc_sem.at[1, 3]),
    )
    for copy in small + local[0] + local[1]:
        copy.start()
    small[0].wait()
    posbuf[0] = pos_ref[...].astype(jnp.float32)

    def swap(stage):
        return (
            pltpu.make_async_remote_copy(
                k_hbm.at[0, :, head_cols(1 - half, stage)],
                kv.at[stage, 0, 0, 3],
                par_send.at[stage, 0],
                par_recv.at[stage, 0],
                device_id=(sec, mate),
                device_id_type=MESH,
            ),
            pltpu.make_async_remote_copy(
                v_hbm.at[0, :, head_cols(1 - half, stage)],
                kv.at[stage, 0, 1, 3],
                par_send.at[stage, 1],
                par_recv.at[stage, 1],
                device_id=(sec, mate),
                device_id_type=MESH,
            ),
            pltpu.make_async_remote_copy(
                q_hbm.at[0, :, wide_cols(1 - half, stage)],
                qbuf.at[stage, pl.ds(ROWS, ROWS), :],
                par_send.at[stage, 2],
                par_recv.at[stage, 2],
                device_id=(sec, mate),
                device_id_type=MESH,
            ),
        )

    def ring_copy(stage, hop, from_piece, piece):
        return pltpu.make_async_remote_copy(
            kv.at[stage, hop, :, from_piece],
            kv.at[stage, hop + 1, :, piece],
            ring_send.at[stage, hop + 1, piece],
            ring_recv.at[stage, hop + 1, piece],
            device_id=toward[piece % 2],
            device_id_type=MESH,
        )

    def pos_copy(from_slot, slot, device):
        return pltpu.make_async_remote_copy(
            posbuf.at[from_slot],
            posbuf.at[slot],
            pos_send.at[slot],
            pos_recv.at[slot],
            device_id=device,
            device_id_type=MESH,
        )

    mate_pos = pos_copy(0, 3, (sec, mate))

    barrier = pltpu.get_barrier_semaphore()
    greeted = (
        (sec, mate),
        (sec, right),
        (sec, left),
        (onward, ctx),
        (onward, mate),
        (behind, ctx),
        (behind, mate),
    )
    for device in greeted:
        pl.semaphore_signal(barrier, inc=1, device_id=device, device_id_type=MESH)
    pl.semaphore_wait(barrier, len(greeted))

    swap_a, swap_b = swap(0), swap(1)
    for copy in (swap_a[0], swap_a[1], mate_pos, swap_b[0], swap_b[1], swap_a[2]):
        copy.start()

    def send(stage, hop, from_piece, piece):
        ring_copy(stage, hop, from_piece, piece).start()

        @pl.when(stage == 0)
        def _():
            pos_copy(4 * hop + from_piece, 4 * hop + 4 + piece, toward[piece % 2]).start()

    def launch(stage, side):
        for way in range(2):
            send(stage, 0, 3 * side, 2 * side + way)

    def take(stage, hop):
        for piece in range(4) if not (isinstance(hop, int) and hop == hops) else (0, 3):
            ring_copy(stage, hop - 1, 0, piece).wait_recv()

            @pl.when(stage == 0)
            def _():
                pos_copy(0, 4 * hop + piece, toward[piece % 2]).wait_recv()

            if isinstance(hop, int):
                if hop < hops - 1 or (hop == hops - 1 and piece in (0, 3)):
                    send(stage, hop, piece, piece)
            elif piece in (0, 3):
                send(stage, hop, piece, piece)
            else:

                @pl.when(hop < hops - 1)
                def _():
                    send(stage, hop, piece, piece)

    for stage in range(STAGES):
        local[stage][0].wait()
        local[stage][1].wait()
        launch(stage, 0)
    for stage, copies in enumerate((swap_a, swap_b)):
        copies[0].wait_recv()
        copies[1].wait_recv()
        if stage == 0:
            mate_pos.wait_recv()
        launch(stage, 1)
    small[1].wait()

    place = jnp.concatenate([posbuf[0], posbuf[3]], axis=1)
    first = jnp.zeros_like(place)
    for doc in range(1, DOCS):
        count = jnp.sum((seg_ref[...] < doc).astype(jnp.float32), axis=0, keepdims=True)
        begin = jnp.sum(count, axis=1, keepdims=True)
        first = jnp.maximum(first, jnp.where(begin <= place, begin, 0.0))
    qrow[0] = place
    qrow[1] = first

    scale = math.log2(math.e) / math.sqrt(HEAD_SIZE)

    def attend(stage, hop, pieces=(0, 1, 2, 3), finish=False):
        width = len(pieces) * ROWS

        @pl.when(stage == 0)
        def _():
            for at, piece in enumerate(pieces):
                spot = jnp.transpose(jnp.broadcast_to(posbuf[4 * hop + piece], (ROWS, ROWS)))
                for side in range(2):
                    lanes = slice(side * ROWS, (side + 1) * ROWS)
                    allowed = (spot <= qrow[0, :, lanes]) & (spot >= qrow[1, :, lanes])
                    bias[hop, at * ROWS : (at + 1) * ROWS, lanes] = jnp.where(allowed, 0.0, NEG)

        for at, piece in enumerate(pieces):
            vt[:, at * ROWS : (at + 1) * ROWS] = jnp.transpose(kv[stage, hop, 1, piece])
        key_rows = jnp.concatenate([kv[stage, hop, 0, piece] for piece in pieces], axis=0)

        def score(head):
            return lax.dot_general(
                key_rows,
                qbuf[stage, :, head * HEAD_SIZE : (head + 1) * HEAD_SIZE],
                (((1,), (1,)), ((), ())),
                preferred_element_type=jnp.float32,
            )

        def soften(head, scores):
            scores = scores * scale + bias[hop, :width]
            old = top[stage, head]
            new = jnp.maximum(old, jnp.max(scores, axis=0, keepdims=True))
            probabilities = jnp.exp2(scores - new)
            factor = jnp.exp2(old - new)
            total[stage, head] = total[stage, head] * factor + jnp.sum(
                probabilities, axis=0, keepdims=True
            )
            top[stage, head] = new
            return probabilities.astype(jnp.bfloat16), factor

        def weigh(head, probabilities, factor):
            weighted = acc[stage, head] * factor + jnp.dot(
                vt[:, :width], probabilities, preferred_element_type=jnp.float32
            )
            if finish:
                result = jnp.transpose(weighted * (1.0 / total[stage, head]))
                obuf[stage, :, head * HEAD_SIZE : (head + 1) * HEAD_SIZE] = result.astype(
                    jnp.bfloat16
                )
                for side in range(2):
                    hand(stage, head, side).start()
            else:
                acc[stage, head] = weighted

        scores, behind_by_one = score(0), None
        for head in range(GROUP):
            following = score(head + 1) if head + 1 < GROUP else None
            softened = soften(head, scores)
            if behind_by_one is not None:
                weigh(head - 1, *behind_by_one)
            scores, behind_by_one = following, softened
        weigh(GROUP - 1, *behind_by_one)

    def hand(stage, head, side):
        spot = pl.multiple_of(((STAGES * half + stage) * GROUP + head) * HEAD_SIZE, HEAD_SIZE)
        return pltpu.make_async_remote_copy(
            obuf.at[stage, pl.ds(side * ROWS, ROWS), pl.ds(head * HEAD_SIZE, HEAD_SIZE)],
            out_hbm.at[0, :, pl.ds(spot, HEAD_SIZE)],
            out_send.at[stage, head, side],
            out_recv.at[stage, head, side],
            device_id=(onward, ctx if side == 0 else mate),
            device_id_type=MESH,
        )

    ends = (0, 3)

    top[...] = jnp.full_like(top, NEG)
    total[...] = jnp.zeros_like(total)
    acc[...] = jnp.zeros_like(acc)
    take(0, 1)
    swap_b[2].start()
    take(1, 1)
    if hops == 8:
        take(0, 2)
        take(1, 2)
        local[0][2].wait()
        swap_a[2].wait_recv()
        attend(0, 0, ends)

        def early(hop, carry):
            attend(0, hop)
            return carry

        lax.fori_loop(1, 3, early, 0)
        take(0, 3)
        local[1][2].wait()
        swap_b[2].wait_recv()
        attend(1, 0, ends)
        attend(1, 1)
        take(1, 3)

        def late(index, carry):
            stage = lax.rem(index, 2)
            hop = index // 2 + 2
            attend(stage, hop)

            @pl.when((index > 1) & (index < 10))
            def _():
                take(stage, hop + 1)

            return carry

        lax.fori_loop(1, 11, late, 0)
        take(0, 8)
        attend(0, 8, ends, finish=True)
        attend(1, 7)
        take(1, 8)
        attend(1, 8, ends, finish=True)
    else:
        local[0][2].wait()
        swap_a[2].wait_recv()
        local[1][2].wait()
        swap_b[2].wait_recv()
        for stage in range(STAGES):
            attend(stage, 0, ends)
        for hop in range(1, hops):
            for stage in range(STAGES):
                attend(stage, hop)
                take(stage, hop + 1)
        for stage in range(STAGES):
            attend(stage, hops, ends, finish=True)

    for copy in swap_a + swap_b + (mate_pos,):
        copy.wait_send()

    def sent(hop, pieces):
        for piece in pieces:
            for stage in range(STAGES):
                ring_copy(stage, hop - 1, 0, piece).wait_send()
            pos_copy(0, 4 * hop + piece, toward[piece % 2]).wait_send()

    def all_sent(hop, carry):
        sent(hop, range(4))
        return carry

    lax.fori_loop(1, hops, all_sent, 0)
    sent(hops, ends)

    for stage in range(STAGES):
        for head in range(GROUP):
            for side in range(2):
                copy = hand(stage, head, side)
                copy.wait_send()
                copy.wait_recv()


def per_device(sections, ring, queries, keys, values, token_pos, segment):
    stay = pl.BlockSpec(memory_space=pltpu.HBM)
    dma = pltpu.SemaphoreType.DMA
    hops = ring // 2
    pairs = ROWS * 2 * ring * ROWS * 2 * QUERY_HEADS // 2
    return pl.pallas_call(
        functools.partial(kernel, sections, ring),
        out_shape=jax.ShapeDtypeStruct(queries.shape, jnp.bfloat16),
        in_specs=[stay] * 5,
        out_specs=pl.BlockSpec(memory_space=pl.ANY),
        scratch_shapes=[
            pltpu.VMEM((STAGES, hops + 1, 2, 4, ROWS, HEAD_SIZE), jnp.bfloat16),
            pltpu.VMEM((STAGES, 2 * ROWS, WIDE), jnp.bfloat16),
            pltpu.VMEM((STAGES, 2 * ROWS, WIDE), jnp.bfloat16),
            pltpu.VMEM((1, ROWS), jnp.int32),
            pltpu.VMEM((ring * ROWS * 2 // 128, 128), jnp.int32),
            pltpu.VMEM((4 * hops + 4, 1, ROWS), jnp.float32),
            pltpu.VMEM((2, 1, 2 * ROWS), jnp.float32),
            pltpu.VMEM((hops + 1, 4 * ROWS, 2 * ROWS), jnp.float32),
            pltpu.VMEM((HEAD_SIZE, 4 * ROWS), jnp.bfloat16),
            pltpu.VMEM((STAGES, GROUP, HEAD_SIZE, 2 * ROWS), jnp.float32),
            pltpu.VMEM((STAGES, GROUP, 1, 2 * ROWS), jnp.float32),
            pltpu.VMEM((STAGES, GROUP, 1, 2 * ROWS), jnp.float32),
            dma((STAGES, 4)),
            dma((STAGES, 3)),
            dma((STAGES, 3)),
            dma((STAGES, hops + 1, 4)),
            dma((STAGES, hops + 1, 4)),
            dma((4 * hops + 4,)),
            dma((4 * hops + 4,)),
            dma((STAGES, GROUP, 2)),
            dma((STAGES, GROUP, 2)),
        ],
        compiler_params=pltpu.CompilerParams(
            collective_id=0, has_side_effects=True, vmem_limit_bytes=40 * 1024 * 1024
        ),
        cost_estimate=pl.CostEstimate(
            flops=4 * HEAD_SIZE * pairs, bytes_accessed=4 * 1024 * 1024, transcendentals=pairs
        ),
    )(
        *(
            pltpu.with_memory_space_constraint(x, pltpu.HBM)
            for x in (queries, keys, values, token_pos.reshape(1, ROWS), segment.reshape(-1, 128))
        )
    )


def solution(mesh):
    return jax.shard_map(
        functools.partial(per_device, mesh.shape["section"], mesh.shape["ctx"] // 2),
        mesh=mesh,
        in_specs=(
            P("section", "ctx", None),
            P("section", "ctx", None),
            P("section", "ctx", None),
            P("ctx"),
            P(),
        ),
        out_specs=P("section", "ctx", None),
        check_vma=False,
    )
```

```python
import functools
import math

import jax
import jax.numpy as jnp
from jax import lax
from jax.experimental import pallas as pl
from jax.experimental.pallas import tpu as pltpu
from jax.sharding import PartitionSpec as P

HEAD_SIZE = 128
QUERY_HEADS = 32
KEY_VALUE_HEADS = 4
DOCS = 8
GROUP = QUERY_HEADS // KEY_VALUE_HEADS
STAGES = KEY_VALUE_HEADS // 2
ROWS = 128
WIDE = GROUP * HEAD_SIZE
NEG = -1e30
MESH = pl.DeviceIdType.MESH


def kernel(
    sections,
    ring,
    q_hbm,
    k_hbm,
    v_hbm,
    pos_hbm,
    seg_hbm,
    out_hbm,
    kv,
    qbuf,
    obuf,
    pos_ref,
    seg_ref,
    posbuf,
    qrow,
    bias,
    vt,
    acc,
    top,
    total,
    loc_sem,
    par_send,
    par_recv,
    ring_send,
    ring_recv,
    pos_send,
    pos_recv,
    out_send,
    out_recv,
):
    hops = ring // 2
    sec = lax.axis_index("section")
    ctx = lax.axis_index("ctx")
    half = lax.rem(ctx, 2)
    mate = ctx + 1 - 2 * half
    right = lax.rem(ctx + 2, 2 * ring)
    left = lax.rem(ctx + 2 * ring - 2, 2 * ring)
    onward = lax.rem(sec + 1, sections)
    behind = lax.rem(sec + sections - 1, sections)
    toward = ((sec, right), (sec, left))

    def head_cols(which_half, stage):
        return pl.ds(pl.multiple_of((STAGES * which_half + stage) * HEAD_SIZE, HEAD_SIZE), HEAD_SIZE)

    def wide_cols(which_half, stage):
        return pl.ds(pl.multiple_of((STAGES * which_half + stage) * WIDE, WIDE), WIDE)

    local = []
    for stage in range(STAGES):
        local.append(
            (
                pltpu.make_async_copy(
                    k_hbm.at[0, :, head_cols(half, stage)], kv.at[stage, 0, 0, 0], loc_sem.at[stage, 0]
                ),
                pltpu.make_async_copy(
                    v_hbm.at[0, :, head_cols(half, stage)], kv.at[stage, 0, 0, 1], loc_sem.at[stage, 1]
                ),
                pltpu.make_async_copy(
                    q_hbm.at[0, :, wide_cols(half, stage)],
                    qbuf.at[stage, pl.ds(0, ROWS), :],
                    loc_sem.at[stage, 2],
                ),
            )
        )
    small = (
        pltpu.make_async_copy(pos_hbm, pos_ref, loc_sem.at[0, 3]),
        pltpu.make_async_copy(seg_hbm, seg_ref, loc_sem.at[1, 3]),
    )
    for copy in small + local[0] + local[1]:
        copy.start()
    small[0].wait()
    posbuf[0] = pos_ref[...].astype(jnp.float32)

    def swap(stage):
        return (
            pltpu.make_async_remote_copy(
                k_hbm.at[0, :, head_cols(1 - half, stage)],
                kv.at[stage, 0, 3, 0],
                par_send.at[stage, 0],
                par_recv.at[stage, 0],
                device_id=(sec, mate),
                device_id_type=MESH,
            ),
            pltpu.make_async_remote_copy(
                v_hbm.at[0, :, head_cols(1 - half, stage)],
                kv.at[stage, 0, 3, 1],
                par_send.at[stage, 1],
                par_recv.at[stage, 1],
                device_id=(sec, mate),
                device_id_type=MESH,
            ),
            pltpu.make_async_remote_copy(
                q_hbm.at[0, :, wide_cols(1 - half, stage)],
                qbuf.at[stage, pl.ds(ROWS, ROWS), :],
                par_send.at[stage, 2],
                par_recv.at[stage, 2],
                device_id=(sec, mate),
                device_id_type=MESH,
            ),
        )

    def ring_copy(stage, hop, from_piece, piece):
        return pltpu.make_async_remote_copy(
            kv.at[stage, hop, from_piece],
            kv.at[stage, hop + 1, piece],
            ring_send.at[stage, hop + 1, piece],
            ring_recv.at[stage, hop + 1, piece],
            device_id=toward[piece % 2],
            device_id_type=MESH,
        )

    def pos_copy(from_slot, slot, device):
        return pltpu.make_async_remote_copy(
            posbuf.at[from_slot],
            posbuf.at[slot],
            pos_send.at[slot],
            pos_recv.at[slot],
            device_id=device,
            device_id_type=MESH,
        )

    mate_pos = pos_copy(0, 3, (sec, mate))

    barrier = pltpu.get_barrier_semaphore()
    greeted = (
        (sec, mate),
        (sec, right),
        (sec, left),
        (onward, ctx),
        (onward, mate),
        (behind, ctx),
        (behind, mate),
    )
    for device in greeted:
        pl.semaphore_signal(barrier, inc=1, device_id=device, device_id_type=MESH)
    pl.semaphore_wait(barrier, len(greeted))

    swap_a, swap_b = swap(0), swap(1)
    for copy in (swap_a[0], swap_a[1], mate_pos, swap_b[0], swap_b[1], swap_a[2]):
        copy.start()

    def send(stage, hop, from_piece, piece):
        ring_copy(stage, hop, from_piece, piece).start()

        @pl.when(stage == 0)
        def _():
            pos_copy(4 * hop + from_piece, 4 * hop + 4 + piece, toward[piece % 2]).start()

    def launch(stage, side):
        for way in range(2):
            send(stage, 0, 3 * side, 2 * side + way)

    def take(stage, hop):
        for piece in range(4) if not (isinstance(hop, int) and hop == hops) else (0, 3):
            ring_copy(stage, hop - 1, 0, piece).wait_recv()

            @pl.when(stage == 0)
            def _():
                pos_copy(0, 4 * hop + piece, toward[piece % 2]).wait_recv()

            if isinstance(hop, int):
                if hop < hops - 1 or (hop == hops - 1 and piece in (0, 3)):
                    send(stage, hop, piece, piece)
            elif piece in (0, 3):
                send(stage, hop, piece, piece)
            else:

                @pl.when(hop < hops - 1)
                def _():
                    send(stage, hop, piece, piece)

    for stage in range(STAGES):
        local[stage][0].wait()
        local[stage][1].wait()
        launch(stage, 0)
    for stage, copies in enumerate((swap_a, swap_b)):
        copies[0].wait_recv()
        copies[1].wait_recv()
        if stage == 0:
            mate_pos.wait_recv()
        launch(stage, 1)
    small[1].wait()

    place = jnp.concatenate([posbuf[0], posbuf[3]], axis=1)
    first = jnp.zeros_like(place)
    for doc in range(1, DOCS):
        count = jnp.sum((seg_ref[...] < doc).astype(jnp.float32), axis=0, keepdims=True)
        begin = jnp.sum(count, axis=1, keepdims=True)
        first = jnp.maximum(first, jnp.where(begin <= place, begin, 0.0))
    qrow[0] = place
    qrow[1] = first

    scale = math.log2(math.e) / math.sqrt(HEAD_SIZE)

    def attend(stage, hop, pieces=(0, 1, 2, 3), finish=False):
        width = len(pieces) * ROWS

        @pl.when(stage == 0)
        def _():
            for at, piece in enumerate(pieces):
                spot = jnp.transpose(jnp.broadcast_to(posbuf[4 * hop + piece], (ROWS, ROWS)))
                for side in range(2):
                    lanes = slice(side * ROWS, (side + 1) * ROWS)
                    allowed = (spot <= qrow[0, :, lanes]) & (spot >= qrow[1, :, lanes])
                    bias[hop, at * ROWS : (at + 1) * ROWS, lanes] = jnp.where(allowed, 0.0, NEG)

        for at, piece in enumerate(pieces):
            vt[:, at * ROWS : (at + 1) * ROWS] = jnp.transpose(kv[stage, hop, piece, 1])
        key_rows = jnp.concatenate([kv[stage, hop, piece, 0] for piece in pieces], axis=0)

        def score(head):
            return lax.dot_general(
                key_rows,
                qbuf[stage, :, head * HEAD_SIZE : (head + 1) * HEAD_SIZE],
                (((1,), (1,)), ((), ())),
                preferred_element_type=jnp.float32,
            )

        def soften(head, scores):
            scores = scores * scale + bias[hop, :width]
            old = top[stage, head]
            new = jnp.maximum(old, jnp.max(scores, axis=0, keepdims=True))
            probabilities = jnp.exp2(scores - new)
            factor = jnp.exp2(old - new)
            total[stage, head] = total[stage, head] * factor + jnp.sum(
                probabilities, axis=0, keepdims=True
            )
            top[stage, head] = new
            return probabilities.astype(jnp.bfloat16), factor

        def weigh(head, probabilities, factor):
            weighted = acc[stage, head] * factor + jnp.dot(
                vt[:, :width], probabilities, preferred_element_type=jnp.float32
            )
            if finish:
                result = jnp.transpose(weighted * (1.0 / total[stage, head]))
                obuf[stage, :, head * HEAD_SIZE : (head + 1) * HEAD_SIZE] = result.astype(
                    jnp.bfloat16
                )
                for side in range(2):
                    hand(stage, head, side).start()
            else:
                acc[stage, head] = weighted

        scores, behind_by_one = score(0), None
        for head in range(GROUP):
            following = score(head + 1) if head + 1 < GROUP else None
            softened = soften(head, scores)
            if behind_by_one is not None:
                weigh(head - 1, *behind_by_one)
            scores, behind_by_one = following, softened
        weigh(GROUP - 1, *behind_by_one)

    def hand(stage, head, side):
        spot = pl.multiple_of(((STAGES * half + stage) * GROUP + head) * HEAD_SIZE, HEAD_SIZE)
        return pltpu.make_async_remote_copy(
            obuf.at[stage, pl.ds(side * ROWS, ROWS), pl.ds(head * HEAD_SIZE, HEAD_SIZE)],
            out_hbm.at[0, :, pl.ds(spot, HEAD_SIZE)],
            out_send.at[stage, head, side],
            out_recv.at[stage, head, side],
            device_id=(onward, ctx if side == 0 else mate),
            device_id_type=MESH,
        )

    ends = (0, 3)

    top[...] = jnp.full_like(top, NEG)
    total[...] = jnp.zeros_like(total)
    acc[...] = jnp.zeros_like(acc)
    take(0, 1)
    swap_b[2].start()
    if hops == 8:
        take(0, 2)
        take(1, 1)
        local[0][2].wait()
        swap_a[2].wait_recv()
        attend(0, 0, ends)

        def early(hop, carry):
            attend(0, hop)

            @pl.when(hop == 2)
            def _():
                take(0, 3)

            return carry

        lax.fori_loop(1, 4, early, 0)
        take(1, 2)
        local[1][2].wait()
        swap_b[2].wait_recv()
        attend(1, 0, ends)

        def middle(index, carry):
            stage = 1 - lax.rem(index, 3) * (2 - lax.rem(index, 3))
            attend(stage, (1 - stage) * 4 + stage * (1 + index // 2 + index // 3))

            @pl.when(index == 0)
            def _():
                take(0, 4)

            @pl.when(index == 1)
            def _():
                take(1, 3)

            return carry

        lax.fori_loop(0, 4, middle, 0)

        def late(index, carry):
            stage = lax.rem(index, 2)
            hop = 5 + index // 2 - stage
            take(stage, hop)
            attend(stage, hop)
            return carry

        lax.fori_loop(0, 6, late, 0)
        take(0, 8)
        attend(0, 8, ends, finish=True)
        take(1, 7)

        def rest(hop, carry):
            attend(1, hop)
            return carry

        lax.fori_loop(7, 8, rest, 0)
        take(1, 8)
        attend(1, 8, ends, finish=True)
    else:
        take(1, 1)
        local[0][2].wait()
        swap_a[2].wait_recv()
        local[1][2].wait()
        swap_b[2].wait_recv()
        for stage in range(STAGES):
            attend(stage, 0, ends)
        for hop in range(1, hops):
            for stage in range(STAGES):
                attend(stage, hop)
                take(stage, hop + 1)
        for stage in range(STAGES):
            attend(stage, hops, ends, finish=True)

    for copy in swap_a + swap_b + (mate_pos,):
        copy.wait_send()

    def sent(hop, pieces):
        for piece in pieces:
            for stage in range(STAGES):
                ring_copy(stage, hop - 1, 0, piece).wait_send()
            pos_copy(0, 4 * hop + piece, toward[piece % 2]).wait_send()

    def all_sent(hop, carry):
        sent(hop, range(4))
        return carry

    lax.fori_loop(1, hops, all_sent, 0)
    sent(hops, ends)

    for stage in range(STAGES):
        for head in range(GROUP):
            for side in range(2):
                copy = hand(stage, head, side)
                copy.wait_send()
                copy.wait_recv()


def per_device(sections, ring, queries, keys, values, token_pos, segment):
    stay = pl.BlockSpec(memory_space=pltpu.HBM)
    dma = pltpu.SemaphoreType.DMA
    hops = ring // 2
    pairs = ROWS * 2 * ring * ROWS * 2 * QUERY_HEADS // 2
    return pl.pallas_call(
        functools.partial(kernel, sections, ring),
        out_shape=jax.ShapeDtypeStruct(queries.shape, jnp.bfloat16),
        in_specs=[stay] * 5,
        out_specs=pl.BlockSpec(memory_space=pl.ANY),
        scratch_shapes=[
            pltpu.VMEM((STAGES, hops + 1, 4, 2, ROWS, HEAD_SIZE), jnp.bfloat16),
            pltpu.VMEM((STAGES, 2 * ROWS, WIDE), jnp.bfloat16),
            pltpu.VMEM((STAGES, 2 * ROWS, WIDE), jnp.bfloat16),
            pltpu.VMEM((1, ROWS), jnp.int32),
            pltpu.VMEM((ring * ROWS * 2 // 128, 128), jnp.int32),
            pltpu.VMEM((4 * hops + 4, 1, ROWS), jnp.float32),
            pltpu.VMEM((2, 1, 2 * ROWS), jnp.float32),
            pltpu.VMEM((hops + 1, 4 * ROWS, 2 * ROWS), jnp.float32),
            pltpu.VMEM((HEAD_SIZE, 4 * ROWS), jnp.bfloat16),
            pltpu.VMEM((STAGES, GROUP, HEAD_SIZE, 2 * ROWS), jnp.float32),
            pltpu.VMEM((STAGES, GROUP, 1, 2 * ROWS), jnp.float32),
            pltpu.VMEM((STAGES, GROUP, 1, 2 * ROWS), jnp.float32),
            dma((STAGES, 4)),
            dma((STAGES, 3)),
            dma((STAGES, 3)),
            dma((STAGES, hops + 1, 4)),
            dma((STAGES, hops + 1, 4)),
            dma((4 * hops + 4,)),
            dma((4 * hops + 4,)),
            dma((STAGES, GROUP, 2)),
            dma((STAGES, GROUP, 2)),
        ],
        compiler_params=pltpu.CompilerParams(
            collective_id=0, has_side_effects=True, vmem_limit_bytes=40 * 1024 * 1024
        ),
        cost_estimate=pl.CostEstimate(
            flops=4 * HEAD_SIZE * pairs, bytes_accessed=4 * 1024 * 1024, transcendentals=pairs
        ),
    )(
        *(
            pltpu.with_memory_space_constraint(x, pltpu.HBM)
            for x in (queries, keys, values, token_pos.reshape(1, ROWS), segment.reshape(-1, 128))
        )
    )


def solution(mesh):
    return jax.shard_map(
        functools.partial(per_device, mesh.shape["section"], mesh.shape["ctx"] // 2),
        mesh=mesh,
        in_specs=(
            P("section", "ctx", None),
            P("section", "ctx", None),
            P("section", "ctx", None),
            P("ctx"),
            P(),
        ),
        out_specs=P("section", "ctx", None),
        check_vma=False,
    )
```
